32 devices in a mesh: row: 4 (over y, x), col: 8 (over z, core).
Axes of the slice: x: 2, y: 2, z: 4, core: 2. Of those that a mesh axis runs over, the one named last changes fastest.
Arguments:
- right_side: float32 [512, 128], P('row'), may hold values from -6 to 6
- factor_window: float32 [512, 512], P('row', 'col'), may hold values from -0.1875 to 0.1875
- diag_inverse: float32 [512, 128], P('row'), as said below
- phase_cov: bfloat16 [512, 16384], P('col', 'row'), may hold values from -0.25 to 0.25
Outputs:
- basis: float32 [32, 512, 128], P('row', 'col')
- solved: float32 [512, 128], P('col')
The draws below stay inside these ranges and needn't reach their ends.
Inputs may be any that keep to these rules, and one draw needn't show every extreme that they name: `diag_inverse`: each block of 128 rows is a lower triangular matrix with a diagonal between 0.5 and 2.
All inputs are finite; a program needn't handle non-finite values.
Results may differ from the reference program's by a relative error of at most 0.0043.
Values sent between devices are 32-bit elements; how exact they have to be, the bound alone decides.
A program may use at most 64 MiB of HBM per device.

```python
import jax
import jax.numpy as jnp
from jax import lax

ROWS_DEV = 128
RANK = 128
TILE_ROWS = 512
K = 512
TILES_ALL = 32
PHASE = 16384
N_ROW = 4


def draw_diag_inverse(key, part):
    first, second = jax.random.split(jax.random.fold_in(key, 7), 2)
    diagonal = jax.random.uniform(first, (K,), jnp.float32, 0.5, 2.0)
    offdiag = 0.5 * jax.random.normal(second, (K, ROWS_DEV), jnp.float32) / jnp.sqrt(jnp.float32(ROWS_DEV))
    local_row = (jnp.arange(K) % ROWS_DEV)[:, None]
    columns = jnp.arange(ROWS_DEV)[None, :]
    return jnp.where(columns < local_row, offdiag, 0.0) + jnp.where(columns == local_row, diagonal[:, None], 0.0)


def levels(stream_key, dims, cuts, smallest, high):
    def one(dim, shards_of):
        steps = jax.random.uniform(jax.random.fold_in(jax.random.fold_in(stream_key, 6), dim), (shards_of,), jnp.float32, smallest / len(cuts), high / len(cuts))
        return jnp.repeat(jnp.exp(steps), dims[dim] // shards_of).reshape((-1,) + (1,) * (len(dims) - dim - 1))

    gain = one(*cuts[0])
    for cut in cuts[1:]:
        gain = gain * one(*cut)
    return gain


def scatter_about(own_key, shape, scale, most, cuts=(), held_as=jnp.bfloat16):
    result = scale * jax.random.normal(own_key, shape, jnp.float32)
    if cuts:
        result = result * levels(own_key, shape, cuts, -0.22, 0.18)
    return jnp.clip(result, -most, most).astype(held_as)


def setup_inputs(seed: int = 0) -> dict:
    streams_of = jax.random.split(jax.random.key(seed), 5)
    right_side = scatter_about(streams_of[0], (K, RANK), 1.0, 6.0, ((0, 4),), jnp.float32)
    factor_window = scatter_about(streams_of[1], (K, K), (2 * K) ** -0.5, 0.1875, ((0, 4), (1, 8)), jnp.float32)
    diag_inverse = draw_diag_inverse(jax.random.fold_in(streams_of[4], 71), 0)
    phase_cov = scatter_about(streams_of[3], (K, PHASE), K ** -0.5, 0.25, ((0, 8), (1, 4)))
    return {"right_side": right_side, "factor_window": factor_window, "diag_inverse": diag_inverse, "phase_cov": phase_cov}


def tile_basis(lower, tile):
    return jax.scipy.linalg.solve_triangular(lower, tile.T, lower=True).T

def reference(right_side, factor_window, diag_inverse, phase_cov):
    pieces = []
    for block_index in range(N_ROW):
        start_row = block_index * ROWS_DEV
        remaining = right_side[start_row:start_row + ROWS_DEV]
        if block_index > 0:
            earlier = jnp.concatenate(pieces, axis=0)
            remaining = remaining - jnp.dot(factor_window[start_row:start_row + ROWS_DEV, :start_row].astype(jnp.float32), earlier.astype(jnp.float32), precision=lax.Precision.HIGHEST, preferred_element_type=jnp.float32)
        pieces.append(jnp.dot(diag_inverse[start_row:start_row + ROWS_DEV].astype(jnp.float32), remaining.astype(jnp.float32), precision=lax.Precision.HIGHEST, preferred_element_type=jnp.float32))
    solved = jnp.concatenate(pieces, axis=0)
    solved_low = solved.astype(jnp.bfloat16)
    weighted = jnp.dot(phase_cov.T.astype(jnp.float32), solved_low.astype(jnp.float32), preferred_element_type=jnp.float32)
    tiles = weighted.reshape(TILES_ALL, TILE_ROWS, RANK)
    gram = jnp.einsum('tsr,tsq->trq', tiles, tiles, precision=lax.Precision.HIGHEST)
    lower = jnp.linalg.cholesky(gram)
    basis = jax.vmap(tile_basis)(lower, tiles)
    return (basis, solved)
```

```python
import functools

import jax
import jax.numpy as jnp
from jax import lax
from jax.experimental import pallas as pl
from jax.experimental.pallas import tpu as pltpu
from jax.sharding import PartitionSpec as P

MESH = pl.DeviceIdType.MESH
CORES = 2
SUB = 8
F32 = jnp.float32
dot_exact = functools.partial(lax.dot_general, precision=lax.Precision.HIGHEST, preferred_element_type=F32)
NN = (((1,), (0,)), ((), ()))
NT = (((1,), (1,)), ((), ()))


def halves(x):
    high = x.astype(jnp.bfloat16)
    return high, (x - high.astype(F32)).astype(jnp.bfloat16)


def dot_low(a, b):
    return lax.dot_general(a, b, NT, preferred_element_type=F32)


def factor_inverse(gram):
    size = gram.shape[0]
    groups = size // SUB
    parts = [gram[g * SUB:(g + 1) * SUB, :] for g in range(groups)]
    lane = lax.broadcasted_iota(jnp.int32, (SUB, size), 1)
    sub = lax.broadcasted_iota(jnp.int32, (SUB, size), 0)
    spread = lambda x: jnp.broadcast_to(x, (SUB, size))
    out = []
    for g0 in range(groups):
        base = g0 * SUB
        inside = (lane >= base) & (lane < base + SUB)
        cols = [spread(parts[g0][:, base + j:base + j + 1]) for j in range(SUB)]
        entry = {(i, j): spread(cols[j][i:i + 1, :]) for i in range(SUB) for j in range(i + 1)}
        lines = [jnp.where(inside, jnp.where(lane == base + j, 1.0, 0.0), spread(parts[g0][j:j + 1, :])) for j in range(SUB)]
        ratio, inverses = {}, []
        for j in range(SUB):
            inverse = 1.0 / entry[j, j]
            inverses.append(inverse)
            for l in range(j + 1, SUB):
                ratio[l, j] = entry[l, j] * inverse
            for l in range(j + 1, SUB):
                for i in range(l, SUB):
                    entry[i, l] = entry[i, l] - entry[i, j] * ratio[l, j]
                lines[l] = lines[l] - ratio[l, j] * lines[j]
        scaled = [lines[j] * inverses[j] for j in range(SUB)]
        for g in range(g0 + 1, groups):
            left = [spread(parts[g][:, base + j:base + j + 1]) for j in range(SUB)]
            value = jnp.where(inside, 0.0, parts[g])
            for j in range(SUB):
                for l in range(j + 1, SUB):
                    left[l] = left[l] - left[j] * ratio[l, j]
                value = value - left[j] * scaled[j]
            parts[g] = value
        done, pivot = lines[0], entry[0, 0]
        for j in range(1, SUB):
            done = jnp.where(sub == j, lines[j], done)
            pivot = jnp.where(sub == j, entry[j, j], pivot)
        out.append(jnp.where(lane <= sub + base, done * lax.rsqrt(pivot), 0.0))
    return jnp.concatenate(out, axis=0)


def kernel(n_row, n_col, rs_ref, fw_ref, di_ref, cov_ref, basis_ref, solved_ref,
           cov_low, cov32, tile, rows, solved_all, low, part, far_part, bases, wide,
           cov_load, cov_send, cov_recv, f_send, f_recv, x_send, x_recv, p_send, p_recv, s_send, s_recv, b_send, b_recv):
    row = lax.axis_index("row")
    col = lax.axis_index("col")
    chips = n_col // CORES
    chip, core = col // CORES, col % CORES
    partner = chip * CORES + (1 - core)
    mirror = chips - 1 - chip
    side = chip // (chips // 2)
    quarter = chips // 4
    block = rs_ref.shape[0]
    width = fw_ref.shape[0]
    piece = cov32.shape[2]
    out_rows = bases.shape[1]
    near = n_col // 2

    def summed(q, k):
        return (k == CORES - 1) & (q >= quarter) & (q < chips - quarter)

    def needed(i, q):
        return q * CORES * width < i * block

    load = pltpu.make_async_copy(cov_ref, cov_low, cov_load)
    load.start()
    barrier = pltpu.get_barrier_semaphore()
    for d in range(1, n_row):
        pl.semaphore_signal(barrier, inc=1, device_id=(lax.rem(row + d, n_row), col), device_id_type=MESH)
    for d in range(1, n_col):
        pl.semaphore_signal(barrier, inc=1, device_id=(row, lax.rem(col + d, n_col)), device_id_type=MESH)

    di = di_ref[...]
    rows[row, pl.ds(0, block), :] = dot_exact(rs_ref[...].T, di, NT)
    rows[row, pl.ds(block + col * width, width), :] = dot_exact(fw_ref[...], di, NT)
    load.wait()
    for t in range(n_col):
        cov32[t] = cov_low[:, t * piece:(t + 1) * piece].astype(F32)
    pl.semaphore_wait(barrier, n_row + n_col - 2)

    def view(i, q, k):
        if isinstance(q, int) and q == chips:
            size = block // CORES
            return rows.at[i, pl.ds(pl.multiple_of(k * size, SUB), size)]
        return rows.at[i, pl.ds(pl.multiple_of(block + (q * CORES + k) * width, SUB), width)]

    def f_copy(q, target, n):
        return pltpu.make_async_remote_copy(
            src_ref=view(row, q, core), dst_ref=view(row, q, core), send_sem=f_send.at[n], recv_sem=f_recv.at[q],
            device_id=(row, target * CORES + core), device_id_type=MESH)

    def x_copy(i, q, d):
        return pltpu.make_async_remote_copy(
            src_ref=view(i, q, core), dst_ref=view(i, q, core), send_sem=x_send.at[d, q], recv_sem=x_recv.at[i, q],
            device_id=(lax.rem(row + d, n_row), col), device_id_type=MESH)

    def p_copy(i, q, k):
        return pltpu.make_async_remote_copy(
            src_ref=view(i, q, k), dst_ref=view(i, q, k), send_sem=p_send.at[i, q], recv_sem=p_recv.at[i, q],
            device_id=(row, partner), device_id_type=MESH)

    far_first = sorted(range(1, n_row), key=lambda d: abs(2 * d - n_row))
    away = sorted(range(1, chips), key=lambda d: abs(2 * d - chips))

    @pl.when(needed(row, chip))
    def _():
        for d in away:
            f_copy(chip, lax.rem(chip + d, chips), d).start()
        for d in far_first:
            x_copy(row, chip, d).start()
        p_copy(row, chip, core).start()
    for d in far_first:
        x_copy(row, chips, d).start()

    def cov_copy(q, k, n):
        via = summed(q, k) & (q // (chips // 2) != side)
        target = jnp.where(via, chips - 1 - q, q) * CORES + k
        slot = lax.rem(col + jnp.where(via, near, 0), n_col)
        return target, pltpu.make_async_remote_copy(
            src_ref=cov32.at[q * CORES + k], dst_ref=tile.at[slot],
            send_sem=cov_send.at[n], recv_sem=cov_recv.at[slot],
            device_id=(row, target), device_id_type=MESH)

    order = [(lax.rem(chip + d, chips), k) for d in away for k in reversed(range(CORES))] + [(chip, 1 - core)]
    cov_sends = [cov_copy(q, k, n) for n, (q, k) in enumerate(order)]
    for target, copy in cov_sends:
        @pl.when(target != col)
        def _():
            copy.start()
    is_summed = summed(chip, core)
    opposite = lax.rem(col + near, n_col)
    tile[col] = cov32[col]

    @pl.when(is_summed)
    def _():
        tile[opposite] = cov32[mirror * CORES + core]

    useful = [q for q in reversed(range(chips)) if needed(n_row - 1, q)]
    for q in useful:
        @pl.when(needed(row, q) & (chip != q))
        def _():
            f_copy(q, chip, 0).wait_recv()
            for d in far_first:
                x_copy(row, q, d).start()
            p_copy(row, q, core).start()

    def pieces(i):
        return [chips] + [q for q in useful if needed(i, q)]

    for i in range(n_row):
        @pl.when(row != i)
        def _():
            for q in pieces(i):
                x_copy(i, q, 1).wait_recv()
                p_copy(i, q, core).start()

    solved = []
    for i in range(n_row):
        for q in pieces(i):
            if q < chips:
                p_copy(i, q, 1 - core).wait_recv()
            else:
                @pl.when(row != i)
                def _():
                    p_copy(i, q, 1 - core).wait_recv()

        value = rows[i, pl.ds(0, block), :]
        if i:
            earlier = jnp.concatenate(solved, axis=1) if i > 1 else solved[0]
            value = value - dot_exact(earlier, rows[i, pl.ds(block, i * block), :], NN)
        solved.append(value)
        solved_all[pl.ds(i * block, block), :] = value.T
    middle = n_row // 2
    low[0] = jnp.concatenate(solved[:middle], axis=1).astype(jnp.bfloat16)
    low[1] = jnp.concatenate(solved[middle:], axis=1).astype(jnp.bfloat16)
    solved_ref[...] = solved_all[pl.ds(pl.multiple_of(col * width, width), width), :]

    def contribution(which, base):
        for j in range(near):
            slot = base + j

            @pl.when((slot != col) & jnp.logical_not(is_summed & (slot == opposite)))
            def _():
                pltpu.make_async_remote_copy(
                    src_ref=cov32.at[slot], dst_ref=tile.at[slot], send_sem=cov_send.at[0], recv_sem=cov_recv.at[slot],
                    device_id=(row, partner), device_id_type=MESH).wait_recv()
        whole = tile[pl.ds(base, near)].reshape(near * width, piece).astype(jnp.bfloat16)
        return lax.dot_general(low[which], whole, NN, preferred_element_type=F32)

    extra = jnp.where(is_summed, 1, 0)
    first = lax.rem(side + extra, 2)
    sum_copy = pltpu.make_async_remote_copy(
        src_ref=part, dst_ref=far_part, send_sem=s_send, recv_sem=s_recv,
        device_id=(row, mirror * CORES + core), device_id_type=MESH)
    part[...] = contribution(side, first * near)

    @pl.when(is_summed)
    def _():
        sum_copy.start()

    @pl.when(jnp.logical_not(is_summed))
    def _():
        far_part[...] = part[...]
    rest = contribution(lax.rem(side + 1 - extra, 2), (1 - first) * near)

    @pl.when(is_summed)
    def _():
        sum_copy.wait_recv()
    weighted = rest + far_part[...]
    wide[...] = weighted.T
    inverse = factor_inverse(dot_exact(weighted, weighted, NT))
    inverse_high, inverse_low = halves(inverse)

    def b_copy(source, target, n):
        return pltpu.make_async_remote_copy(
            src_ref=bases.at[target], dst_ref=basis_ref.at[source],
            send_sem=b_send.at[n], recv_sem=b_recv.at[source],
            device_id=(row, target), device_id_type=MESH)

    def basis_rows(targets):
        taken = jnp.concatenate([wide[pl.ds(pl.multiple_of(t * out_rows, out_rows), out_rows), :] for t in targets], axis=0)
        high, low_half = halves(taken)
        found = dot_low(high, inverse_high) + (dot_low(high, inverse_low) + dot_low(low_half, inverse_high))
        return [found[j * out_rows:(j + 1) * out_rows, :] for j in range(len(targets))]

    peers = [q * CORES + k for q, k in order]
    b_sends = []
    for chosen in (peers[:near], peers[near:]):
        found = basis_rows(chosen if len(chosen) == near else chosen + [col])
        for target, value in zip(chosen, found):
            bases[target] = value
        for target in chosen:
            copy = b_copy(col, target, len(b_sends))
            copy.start()
            b_sends.append(copy)
        if len(found) > len(chosen):
            basis_ref[col] = found[-1]
    for target, copy in cov_sends:
        @pl.when(target != col)
        def _():
            copy.wait_send()

    @pl.when(is_summed)
    def _():
        sum_copy.wait_send()

    @pl.when(needed(row, chip))
    def _():
        for d in away:
            f_copy(chip, chip, d).wait_send()
    for d in far_first:
        x_copy(row, chips, d).wait_send()
    for q in useful:
        @pl.when(needed(row, q))
        def _():
            for d in far_first:
                x_copy(row, q, d).wait_send()
            p_copy(row, q, core).wait_send()
    for i in range(n_row):
        @pl.when(row != i)
        def _():
            for q in pieces(i):
                p_copy(i, q, core).wait_send()
    for n, source in enumerate(peers):
        b_copy(source, col, n).wait_recv()
    for copy in b_sends:
        copy.wait_send()


def solution(mesh):
    n_row, n_col = mesh.shape["row"], mesh.shape["col"]

    def local(right_side, factor_window, diag_inverse, phase_cov):
        block, rank = right_side.shape
        width = factor_window.shape[1]
        chips = n_col // CORES
        piece = phase_cov.shape[1] // n_col
        out_rows = piece // n_col
        vmem = pl.BlockSpec(memory_space=pltpu.VMEM)
        dma = pltpu.SemaphoreType.DMA
        return pl.pallas_call(
            functools.partial(kernel, n_row, n_col),
            out_shape=(
                pltpu.VMEM((n_col, out_rows, rank), F32),
                pltpu.VMEM((width, rank), F32),
            ),
            in_specs=[vmem] * 3 + [pl.BlockSpec(memory_space=pl.ANY)],
            out_specs=(vmem, vmem),
            scratch_shapes=[
                pltpu.VMEM(phase_cov.shape, phase_cov.dtype),
                pltpu.VMEM((n_col, width, piece), F32),
                pltpu.VMEM((n_col, width, piece), F32),
                pltpu.VMEM((n_row, (n_row + 1) * block, rank), F32),
                pltpu.VMEM((n_row * block, rank), F32),
                pltpu.VMEM((2, rank, n_row * block // 2), jnp.bfloat16),
                pltpu.VMEM((rank, piece), F32),
                pltpu.VMEM((rank, piece), F32),
                pltpu.VMEM((n_col, out_rows, rank), F32),
                pltpu.VMEM((piece, rank), F32),
                dma, dma((n_col,)), dma((n_col,)),
                dma((chips,)), dma((chips,)),
                dma((n_row, chips + 1)), dma((n_row, chips + 1)), dma((n_row, chips + 1)), dma((n_row, chips + 1)),
                dma, dma, dma((n_col,)), dma((n_col,)),
            ],
            compiler_params=pltpu.CompilerParams(collective_id=0, has_side_effects=True),
        )(right_side, factor_window.T, diag_inverse, phase_cov)

    in_specs = (P("row", None), P("row", "col"), P("row", None), P("col", "row"))
    out_specs = (P("row", "col", None), P("col", None))
    return jax.shard_map(local, mesh=mesh, in_specs=in_specs, out_specs=out_specs, check_vma=False)
```

```python
import functools

import jax
import jax.numpy as jnp
from jax import lax
from jax.experimental import pallas as pl
from jax.experimental.pallas import tpu as pltpu
from jax.sharding import PartitionSpec as P

MESH = pl.DeviceIdType.MESH
CORES = 2
SUB = 8
F32 = jnp.float32
dot_exact = functools.partial(lax.dot_general, precision=lax.Precision.HIGHEST, preferred_element_type=F32)
NN = (((1,), (0,)), ((), ()))
NT = (((1,), (1,)), ((), ()))


def halves(x):
    high = x.astype(jnp.bfloat16)
    return high, (x - high.astype(F32)).astype(jnp.bfloat16)


def dot_low(a, b):
    return lax.dot_general(a, b, NT, preferred_element_type=F32)


def factor_inverse(gram):
    size = gram.shape[0]
    groups = size // SUB
    parts = [gram[g * SUB:(g + 1) * SUB, :] for g in range(groups)]
    lane = lax.broadcasted_iota(jnp.int32, (SUB, size), 1)
    sub = lax.broadcasted_iota(jnp.int32, (SUB, size), 0)
    spread = lambda x: jnp.broadcast_to(x, (SUB, size))
    out = []
    for g0 in range(groups):
        base = g0 * SUB
        inside = (lane >= base) & (lane < base + SUB)
        cols = [spread(parts[g0][:, base + j:base + j + 1]) for j in range(SUB)]
        entry = {(i, j): spread(cols[j][i:i + 1, :]) for i in range(SUB) for j in range(i + 1)}
        lines = [jnp.where(inside, jnp.where(lane == base + j, 1.0, 0.0), spread(parts[g0][j:j + 1, :])) for j in range(SUB)]
        ratio, inverses = {}, []
        for j in range(SUB):
            inverse = 1.0 / entry[j, j]
            inverses.append(inverse)
            for l in range(j + 1, SUB):
                ratio[l, j] = entry[l, j] * inverse
            for l in range(j + 1, SUB):
                for i in range(l, SUB):
                    entry[i, l] = entry[i, l] - entry[i, j] * ratio[l, j]
                lines[l] = lines[l] - ratio[l, j] * lines[j]
        scaled = [lines[j] * inverses[j] for j in range(SUB)]
        for g in range(g0 + 1, groups):
            left = [spread(parts[g][:, base + j:base + j + 1]) for j in range(SUB)]
            value = jnp.where(inside, 0.0, parts[g])
            for j in range(SUB):
                for l in range(j + 1, SUB):
                    left[l] = left[l] - left[j] * ratio[l, j]
                value = value - left[j] * scaled[j]
            parts[g] = value
        done, pivot = lines[0], entry[0, 0]
        for j in range(1, SUB):
            done = jnp.where(sub == j, lines[j], done)
            pivot = jnp.where(sub == j, entry[j, j], pivot)
        out.append(jnp.where(lane <= sub + base, done * lax.rsqrt(pivot), 0.0))
    return jnp.concatenate(out, axis=0)


def kernel(n_row, n_col, rs_ref, fw_ref, di_ref, cov_ref, basis_ref, solved_ref,
           cov_low, cov32, tile, rows, solved_all, low, part, far_part, bases, wide,
           cov_load, cov_send, cov_recv, f_send, f_recv, x_send, x_recv, p_send, p_recv, s_send, s_recv, b_send, b_recv):
    row = lax.axis_index("row")
    col = lax.axis_index("col")
    chips = n_col // CORES
    chip, core = col // CORES, col % CORES
    partner = chip * CORES + (1 - core)
    mirror = chips - 1 - chip
    side = chip // (chips // 2)
    block = rs_ref.shape[0]
    width = fw_ref.shape[0]
    piece = cov32.shape[2]
    out_rows = bases.shape[1]
    near = n_col // 2

    def summed(q, k):
        return (k == CORES - 1) & (q < chips)

    def needed(i, q):
        return q * CORES * width < i * block

    load = pltpu.make_async_copy(cov_ref, cov_low, cov_load)
    load.start()
    barrier = pltpu.get_barrier_semaphore()
    for d in range(1, n_row):
        pl.semaphore_signal(barrier, inc=1, device_id=(lax.rem(row + d, n_row), col), device_id_type=MESH)
    for d in range(1, n_col):
        pl.semaphore_signal(barrier, inc=1, device_id=(row, lax.rem(col + d, n_col)), device_id_type=MESH)

    di = di_ref[...]
    rows[row, pl.ds(0, block), :] = dot_exact(rs_ref[...].T, di, NT)
    rows[row, pl.ds(block + col * width, width), :] = dot_exact(fw_ref[...], di, NT)
    load.wait()
    for t in range(n_col):
        cov32[t] = cov_low[:, t * piece:(t + 1) * piece].astype(F32)
    pl.semaphore_wait(barrier, n_row + n_col - 2)

    def view(i, q, k):
        if isinstance(q, int) and q == chips:
            size = block // CORES
            return rows.at[i, pl.ds(pl.multiple_of(k * size, SUB), size)]
        return rows.at[i, pl.ds(pl.multiple_of(block + (q * CORES + k) * width, SUB), width)]

    def f_copy(q, target, n):
        return pltpu.make_async_remote_copy(
            src_ref=view(row, q, core), dst_ref=view(row, q, core), send_sem=f_send.at[n], recv_sem=f_recv.at[q],
            device_id=(row, target * CORES + core), device_id_type=MESH)

    def x_copy(i, q, d):
        return pltpu.make_async_remote_copy(
            src_ref=view(i, q, core), dst_ref=view(i, q, core), send_sem=x_send.at[d, q], recv_sem=x_recv.at[i, q],
            device_id=(lax.rem(row + d, n_row), col), device_id_type=MESH)

    def p_copy(i, q, k):
        return pltpu.make_async_remote_copy(
            src_ref=view(i, q, k), dst_ref=view(i, q, k), send_sem=p_send.at[i, q], recv_sem=p_recv.at[i, q],
            device_id=(row, partner), device_id_type=MESH)

    far_first = sorted(range(1, n_row), key=lambda d: abs(2 * d - n_row))
    away = sorted(range(1, chips), key=lambda d: abs(2 * d - chips))

    @pl.when(needed(row, chip))
    def _():
        for d in away:
            f_copy(chip, lax.rem(chip + d, chips), d).start()
        for d in far_first:
            x_copy(row, chip, d).start()
        p_copy(row, chip, core).start()
    for d in far_first:
        x_copy(row, chips, d).start()

    def cov_copy(q, k, n):
        via = summed(q, k) & (q // (chips // 2) != side)
        target = jnp.where(via, chips - 1 - q, q) * CORES + k
        slot = lax.rem(col + jnp.where(via, near, 0), n_col)
        return target, pltpu.make_async_remote_copy(
            src_ref=cov32.at[q * CORES + k], dst_ref=tile.at[slot],
            send_sem=cov_send.at[n], recv_sem=cov_recv.at[slot],
            device_id=(row, target), device_id_type=MESH)

    order = [(lax.rem(chip + d, chips), k) for d in away for k in reversed(range(CORES))] + [(chip, 1 - core)]
    cov_sends = [cov_copy(q, k, n) for n, (q, k) in enumerate(order)]
    for target, copy in cov_sends:
        @pl.when(target != col)
        def _():
            copy.start()
    is_summed = summed(chip, core)
    opposite = lax.rem(col + near, n_col)
    tile[col] = cov32[col]

    @pl.when(is_summed)
    def _():
        tile[opposite] = cov32[mirror * CORES + core]

    useful = [q for q in reversed(range(chips)) if needed(n_row - 1, q)]
    for q in useful:
        @pl.when(needed(row, q) & (chip != q))
        def _():
            f_copy(q, chip, 0).wait_recv()
            for d in far_first:
                x_copy(row, q, d).start()
            p_copy(row, q, core).start()

    def pieces(i):
        return [chips] + [q for q in useful if needed(i, q)]

    for i in range(n_row):
        @pl.when(row != i)
        def _():
            for q in pieces(i):
                x_copy(i, q, 1).wait_recv()
                p_copy(i, q, core).start()

    solved = []
    for i in range(n_row):
        for q in pieces(i):
            if q < chips:
                p_copy(i, q, 1 - core).wait_recv()
            else:
                @pl.when(row != i)
                def _():
                    p_copy(i, q, 1 - core).wait_recv()

        value = rows[i, pl.ds(0, block), :]
        if i:
            earlier = jnp.concatenate(solved, axis=1) if i > 1 else solved[0]
            value = value - dot_exact(earlier, rows[i, pl.ds(block, i * block), :], NN)
        solved.append(value)
        solved_all[pl.ds(i * block, block), :] = value.T
    middle = n_row // 2
    low[0] = jnp.concatenate(solved[:middle], axis=1).astype(jnp.bfloat16)
    low[1] = jnp.concatenate(solved[middle:], axis=1).astype(jnp.bfloat16)
    solved_ref[...] = solved_all[pl.ds(pl.multiple_of(col * width, width), width), :]

    def contribution(which, base):
        for j in range(near):
            slot = base + j

            @pl.when((slot != col) & jnp.logical_not(is_summed & (slot == opposite)))
            def _():
                pltpu.make_async_remote_copy(
                    src_ref=cov32.at[slot], dst_ref=tile.at[slot], send_sem=cov_send.at[0], recv_sem=cov_recv.at[slot],
                    device_id=(row, partner), device_id_type=MESH).wait_recv()
        whole = tile[pl.ds(base, near)].reshape(near * width, piece).astype(jnp.bfloat16)
        return lax.dot_general(low[which], whole, NN, preferred_element_type=F32)

    extra = jnp.where(is_summed, 1, 0)
    first = lax.rem(side + extra, 2)
    sum_copy = pltpu.make_async_remote_copy(
        src_ref=part, dst_ref=far_part, send_sem=s_send, recv_sem=s_recv,
        device_id=(row, mirror * CORES + core), device_id_type=MESH)
    part[...] = contribution(side, first * near)

    @pl.when(is_summed)
    def _():
        sum_copy.start()

    @pl.when(jnp.logical_not(is_summed))
    def _():
        far_part[...] = part[...]
    rest = contribution(lax.rem(side + 1 - extra, 2), (1 - first) * near)

    @pl.when(is_summed)
    def _():
        sum_copy.wait_recv()
    weighted = rest + far_part[...]
    wide[...] = weighted.T
    inverse = factor_inverse(dot_exact(weighted, weighted, NT))
    inverse_high, inverse_low = halves(inverse)

    def b_copy(source, target, n):
        return pltpu.make_async_remote_copy(
            src_ref=bases.at[target], dst_ref=basis_ref.at[source],
            send_sem=b_send.at[n], recv_sem=b_recv.at[source],
            device_id=(row, target), device_id_type=MESH)

    def basis_rows(targets):
        taken = jnp.concatenate([wide[pl.ds(pl.multiple_of(t * out_rows, out_rows), out_rows), :] for t in targets], axis=0)
        high, low_half = halves(taken)
        found = dot_low(high, inverse_high) + (dot_low(high, inverse_low) + dot_low(low_half, inverse_high))
        return [found[j * out_rows:(j + 1) * out_rows, :] for j in range(len(targets))]

    peers = [q * CORES + k for q, k in order]
    b_sends = []
    for chosen in (peers[:near], peers[near:]):
        found = basis_rows(chosen if len(chosen) == near else chosen + [col])
        for target, value in zip(chosen, found):
            bases[target] = value
        for target in chosen:
            copy = b_copy(col, target, len(b_sends))
            copy.start()
            b_sends.append(copy)
        if len(found) > len(chosen):
            basis_ref[col] = found[-1]
    for target, copy in cov_sends:
        @pl.when(target != col)
        def _():
            copy.wait_send()

    @pl.when(is_summed)
    def _():
        sum_copy.wait_send()

    @pl.when(needed(row, chip))
    def _():
        for d in away:
            f_copy(chip, chip, d).wait_send()
    for d in far_first:
        x_copy(row, chips, d).wait_send()
    for q in useful:
        @pl.when(needed(row, q))
        def _():
            for d in far_first:
                x_copy(row, q, d).wait_send()
            p_copy(row, q, core).wait_send()
    for i in range(n_row):
        @pl.when(row != i)
        def _():
            for q in pieces(i):
                p_copy(i, q, core).wait_send()
    for n, source in enumerate(peers):
        b_copy(source, col, n).wait_recv()
    for copy in b_sends:
        copy.wait_send()


def solution(mesh):
    n_row, n_col = mesh.shape["row"], mesh.shape["col"]

    def local(right_side, factor_window, diag_inverse, phase_cov):
        block, rank = right_side.shape
        width = factor_window.shape[1]
        chips = n_col // CORES
        piece = phase_cov.shape[1] // n_col
        out_rows = piece // n_col
        vmem = pl.BlockSpec(memory_space=pltpu.VMEM)
        dma = pltpu.SemaphoreType.DMA
        return pl.pallas_call(
            functools.partial(kernel, n_row, n_col),
            out_shape=(
                pltpu.VMEM((n_col, out_rows, rank), F32),
                pltpu.VMEM((width, rank), F32),
            ),
            in_specs=[vmem] * 3 + [pl.BlockSpec(memory_space=pl.ANY)],
            out_specs=(vmem, vmem),
            scratch_shapes=[
                pltpu.VMEM(phase_cov.shape, phase_cov.dtype),
                pltpu.VMEM((n_col, width, piece), F32),
                pltpu.VMEM((n_col, width, piece), F32),
                pltpu.VMEM((n_row, (n_row + 1) * block, rank), F32),
                pltpu.VMEM((n_row * block, rank), F32),
                pltpu.VMEM((2, rank, n_row * block // 2), jnp.bfloat16),
                pltpu.VMEM((rank, piece), F32),
                pltpu.VMEM((rank, piece), F32),
                pltpu.VMEM((n_col, out_rows, rank), F32),
                pltpu.VMEM((piece, rank), F32),
                dma, dma((n_col,)), dma((n_col,)),
                dma((chips,)), dma((chips,)),
                dma((n_row, chips + 1)), dma((n_row, chips + 1)), dma((n_row, chips + 1)), dma((n_row, chips + 1)),
                dma, dma, dma((n_col,)), dma((n_col,)),
            ],
            compiler_params=pltpu.CompilerParams(collective_id=0, has_side_effects=True),
        )(right_side, factor_window.T, diag_inverse, phase_cov)

    in_specs = (P("row", None), P("row", "col"), P("row", None), P("col", "row"))
    out_specs = (P("row", "col", None), P("col", None))
    return jax.shard_map(local, mesh=mesh, in_specs=in_specs, out_specs=out_specs, check_vma=False)
```

```python
import functools

import jax
import jax.numpy as jnp
from jax import lax
from jax.experimental import pallas as pl
from jax.experimental.pallas import tpu as pltpu
from jax.sharding import PartitionSpec as P

MESH = pl.DeviceIdType.MESH
CORES = 2
SUB = 8
F32 = jnp.float32
dot_exact = functools.partial(lax.dot_general, precision=lax.Precision.HIGHEST, preferred_element_type=F32)
NN = (((1,), (0,)), ((), ()))
NT = (((1,), (1,)), ((), ()))


def halves(x):
    high = x.astype(jnp.bfloat16)
    return high, (x - high.astype(F32)).astype(jnp.bfloat16)


def dot_low(a, b):
    return lax.dot_general(a, b, NT, preferred_element_type=F32)


def factor_inverse(gram):
    size = gram.shape[0]
    groups = size // SUB
    parts = [gram[g * SUB:(g + 1) * SUB, :] for g in range(groups)]
    lane = lax.broadcasted_iota(jnp.int32, (SUB, size), 1)
    sub = lax.broadcasted_iota(jnp.int32, (SUB, size), 0)
    spread = lambda x: jnp.broadcast_to(x, (SUB, size))
    out = []
    for g0 in range(groups):
        base = g0 * SUB
        inside = (lane >= base) & (lane < base + SUB)
        cols = [spread(parts[g0][:, base + j:base + j + 1]) for j in range(SUB)]
        entry = {(i, j): spread(cols[j][i:i + 1, :]) for i in range(SUB) for j in range(i + 1)}
        lines = [jnp.where(inside, jnp.where(lane == base + j, 1.0, 0.0), spread(parts[g0][j:j + 1, :])) for j in range(SUB)]
        ratio, inverses = {}, []
        for j in range(SUB):
            inverse = 1.0 / entry[j, j]
            inverses.append(inverse)
            for l in range(j + 1, SUB):
                ratio[l, j] = entry[l, j] * inverse
            for l in range(j + 1, SUB):
                for i in range(l, SUB):
                    entry[i, l] = entry[i, l] - entry[i, j] * ratio[l, j]
                lines[l] = lines[l] - ratio[l, j] * lines[j]
        scaled = [lines[j] * inverses[j] for j in range(SUB)]
        for g in range(g0 + 1, groups):
            left = [spread(parts[g][:, base + j:base + j + 1]) for j in range(SUB)]
            value = jnp.where(inside, 0.0, parts[g])
            for j in range(SUB):
                for l in range(j + 1, SUB):
                    left[l] = left[l] - left[j] * ratio[l, j]
                value = value - left[j] * scaled[j]
            parts[g] = value
        done, pivot = lines[0], entry[0, 0]
        for j in range(1, SUB):
            done = jnp.where(sub == j, lines[j], done)
            pivot = jnp.where(sub == j, entry[j, j], pivot)
        out.append(jnp.where(lane <= sub + base, done * lax.rsqrt(pivot), 0.0))
    return jnp.concatenate(out, axis=0)


def kernel(n_row, n_col, rs_ref, fw_ref, di_ref, cov_ref, basis_ref, solved_ref,
           cov_low, cov32, tile, rows, solved_all, low, part, far_part, bases, wide,
           cov_load, cov_send, cov_recv, f_send, f_recv, x_send, x_recv, p_send, p_recv, s_send, s_recv, b_send, b_recv):
    row = lax.axis_index("row")
    col = lax.axis_index("col")
    chips = n_col // CORES
    chip, core = col // CORES, col % CORES
    partner = chip * CORES + (1 - core)
    mirror = chips - 1 - chip
    side = chip // (chips // 2)
    block = rs_ref.shape[0]
    width = fw_ref.shape[0]
    piece = cov32.shape[2]
    out_rows = bases.shape[1]
    near = n_col // 2

    def summed(q, k):
        return (k == CORES - 1) & (q < chips)

    def needed(i, q):
        return q * CORES * width < i * block

    load = pltpu.make_async_copy(cov_ref, cov_low, cov_load)
    load.start()
    barrier = pltpu.get_barrier_semaphore()
    for d in range(1, n_row):
        pl.semaphore_signal(barrier, inc=1, device_id=(lax.rem(row + d, n_row), col), device_id_type=MESH)
    for d in range(1, n_col):
        pl.semaphore_signal(barrier, inc=1, device_id=(row, lax.rem(col + d, n_col)), device_id_type=MESH)

    di = di_ref[...]
    rows[row, pl.ds(0, block), :] = dot_exact(rs_ref[...].T, di, NT)
    rows[row, pl.ds(block + col * width, width), :] = dot_exact(fw_ref[...], di, NT)
    load.wait()
    for t in range(n_col):
        cov32[t] = cov_low[:, t * piece:(t + 1) * piece].astype(F32)
    pl.semaphore_wait(barrier, n_row + n_col - 2)

    def view(i, q, k):
        if isinstance(q, int) and q == chips:
            size = block // CORES
            return rows.at[i, pl.ds(pl.multiple_of(k * size, SUB), size)]
        return rows.at[i, pl.ds(pl.multiple_of(block + (q * CORES + k) * width, SUB), width)]

    def f_copy(q, target, n):
        return pltpu.make_async_remote_copy(
            src_ref=view(row, q, core), dst_ref=view(row, q, core), send_sem=f_send.at[n], recv_sem=f_recv.at[q],
            device_id=(row, target * CORES + core), device_id_type=MESH)

    def x_copy(i, q, d):
        return pltpu.make_async_remote_copy(
            src_ref=view(i, q, core), dst_ref=view(i, q, core), send_sem=x_send.at[d, q], recv_sem=x_recv.at[i, q],
            device_id=(lax.rem(row + d, n_row), col), device_id_type=MESH)

    def p_copy(i, q, k):
        return pltpu.make_async_remote_copy(
            src_ref=view(i, q, k), dst_ref=view(i, q, k), send_sem=p_send.at[i, q], recv_sem=p_recv.at[i, q],
            device_id=(row, partner), device_id_type=MESH)

    far_first = sorted(range(1, n_row), key=lambda d: abs(2 * d - n_row))
    away = sorted(range(1, chips), key=lambda d: abs(2 * d - chips))

    @pl.when(needed(row, chip))
    def _():
        for d in away:
            f_copy(chip, lax.rem(chip + d, chips), d).start()
        for d in far_first:
            x_copy(row, chip, d).start()
        p_copy(row, chip, core).start()
    for d in far_first:
        x_copy(row, chips, d).start()

    def cov_copy(q, k, n):
        via = summed(q, k) & (q // (chips // 2) != side)
        target = jnp.where(via, chips - 1 - q, q) * CORES + k
        slot = lax.rem(col + jnp.where(via, near, 0), n_col)
        return target, pltpu.make_async_remote_copy(
            src_ref=cov32.at[q * CORES + k], dst_ref=tile.at[slot],
            send_sem=cov_send.at[n], recv_sem=cov_recv.at[slot],
            device_id=(row, target), device_id_type=MESH)

    def hop(d):
        return sum(lax.rem(chip // b + d // b, 2) * b for b in (2 ** n for n in range(chips)) if b < chips)

    distant = chips // 2
    steps = [*range(distant, chips), *range(1, distant)]
    order = [(hop(d), k) for d in steps for k in reversed(range(CORES))] + [(chip, 1 - core)]
    cov_sends = [cov_copy(q, k, n) for n, (q, k) in enumerate(order)]
    for target, copy in cov_sends:
        @pl.when(target != col)
        def _():
            copy.start()
    is_summed = summed(chip, core)
    opposite = lax.rem(col + near, n_col)
    tile[col] = cov32[col]

    @pl.when(is_summed)
    def _():
        tile[opposite] = cov32[mirror * CORES + core]

    useful = [q for q in reversed(range(chips)) if needed(n_row - 1, q)]
    for q in useful:
        @pl.when(needed(row, q) & (chip != q))
        def _():
            f_copy(q, chip, 0).wait_recv()
            for d in far_first:
                x_copy(row, q, d).start()
            p_copy(row, q, core).start()

    def pieces(i):
        return [chips] + [q for q in useful if needed(i, q)]

    for i in range(n_row):
        @pl.when(row != i)
        def _():
            for q in pieces(i):
                x_copy(i, q, 1).wait_recv()
                p_copy(i, q, core).start()

    solved = []
    for i in range(n_row):
        for q in pieces(i):
            if q < chips:
                p_copy(i, q, 1 - core).wait_recv()
            else:
                @pl.when(row != i)
                def _():
                    p_copy(i, q, 1 - core).wait_recv()

        value = rows[i, pl.ds(0, block), :]
        if i:
            earlier = jnp.concatenate(solved, axis=1) if i > 1 else solved[0]
            value = value - dot_exact(earlier, rows[i, pl.ds(block, i * block), :], NN)
        solved.append(value)
        solved_all[pl.ds(i * block, block), :] = value.T
    middle = n_row // 2
    low[0] = jnp.concatenate(solved[:middle], axis=1).astype(jnp.bfloat16)
    low[1] = jnp.concatenate(solved[middle:], axis=1).astype(jnp.bfloat16)
    solved_ref[...] = solved_all[pl.ds(pl.multiple_of(col * width, width), width), :]

    def contribution(which, base):
        for j in range(near):
            slot = base + j

            @pl.when((slot != col) & jnp.logical_not(is_summed & (slot == opposite)))
            def _():
                pltpu.make_async_remote_copy(
                    src_ref=cov32.at[slot], dst_ref=tile.at[slot], send_sem=cov_send.at[0], recv_sem=cov_recv.at[slot],
                    device_id=(row, partner), device_id_type=MESH).wait_recv()
        whole = tile[pl.ds(base, near)].reshape(near * width, piece).astype(jnp.bfloat16)
        return lax.dot_general(low[which], whole, NN, preferred_element_type=F32)

    extra = jnp.where(is_summed, 1, 0)
    first = lax.rem(side + extra, 2)
    sum_copy = pltpu.make_async_remote_copy(
        src_ref=part, dst_ref=far_part, send_sem=s_send, recv_sem=s_recv,
        device_id=(row, mirror * CORES + core), device_id_type=MESH)
    part[...] = contribution(side, first * near)

    @pl.when(is_summed)
    def _():
        sum_copy.start()

    @pl.when(jnp.logical_not(is_summed))
    def _():
        far_part[...] = part[...]
    rest = contribution(lax.rem(side + 1 - extra, 2), (1 - first) * near)

    @pl.when(is_summed)
    def _():
        sum_copy.wait_recv()
    weighted = rest + far_part[...]
    wide[...] = weighted.T
    inverse = factor_inverse(dot_exact(weighted, weighted, NT))
    inverse_high, inverse_low = halves(inverse)

    def b_copy(source, target, n):
        return pltpu.make_async_remote_copy(
            src_ref=bases.at[target], dst_ref=basis_ref.at[source],
            send_sem=b_send.at[n], recv_sem=b_recv.at[source],
            device_id=(row, target), device_id_type=MESH)

    def basis_rows(targets):
        taken = jnp.concatenate([wide[pl.ds(pl.multiple_of(t * out_rows, out_rows), out_rows), :] for t in targets], axis=0)
        high, low_half = halves(taken)
        found = dot_low(high, inverse_high) + (dot_low(high, inverse_low) + dot_low(low_half, inverse_high))
        return [found[j * out_rows:(j + 1) * out_rows, :] for j in range(len(targets))]

    peers = [hop(d) * CORES + k for d, k in [(d, k) for d in reversed(range(1, chips)) for k in range(CORES)]] + [partner]
    b_sends = []
    for chosen in (peers[:near], peers[near:]):
        found = basis_rows(chosen if len(chosen) == near else chosen + [col])
        for target, value in zip(chosen, found):
            bases[target] = value
        for target in chosen:
            copy = b_copy(col, target, len(b_sends))
            copy.start()
            b_sends.append(copy)
        if len(found) > len(chosen):
            basis_ref[col] = found[-1]
    for target, copy in cov_sends:
        @pl.when(target != col)
        def _():
            copy.wait_send()

    @pl.when(is_summed)
    def _():
        sum_copy.wait_send()

    @pl.when(needed(row, chip))
    def _():
        for d in away:
            f_copy(chip, chip, d).wait_send()
    for d in far_first:
        x_copy(row, chips, d).wait_send()
    for q in useful:
        @pl.when(needed(row, q))
        def _():
            for d in far_first:
                x_copy(row, q, d).wait_send()
            p_copy(row, q, core).wait_send()
    for i in range(n_row):
        @pl.when(row != i)
        def _():
            for q in pieces(i):
                p_copy(i, q, core).wait_send()
    for n, source in enumerate(peers):
        b_copy(source, col, n).wait_recv()
    for copy in b_sends:
        copy.wait_send()


def store(basis_in, solved_in, basis_out, solved_out, sems):
    first = pltpu.make_async_copy(basis_in, basis_out, sems.at[0])
    second = pltpu.make_async_copy(solved_in, solved_out, sems.at[1])
    first.start()
    second.start()
    first.wait()
    second.wait()


def solution(mesh):
    n_row, n_col = mesh.shape["row"], mesh.shape["col"]

    def local(right_side, factor_window, diag_inverse, phase_cov):
        block, rank = right_side.shape
        width = factor_window.shape[1]
        chips = n_col // CORES
        piece = phase_cov.shape[1] // n_col
        out_rows = piece // n_col
        vmem = pl.BlockSpec(memory_space=pltpu.VMEM)
        dma = pltpu.SemaphoreType.DMA
        found = pl.pallas_call(
            functools.partial(kernel, n_row, n_col),
            out_shape=(
                pltpu.VMEM((n_col, out_rows, rank), F32),
                pltpu.VMEM((width, rank), F32),
            ),
            in_specs=[vmem] * 3 + [pl.BlockSpec(memory_space=pl.ANY)],
            out_specs=(vmem, vmem),
            scratch_shapes=[
                pltpu.VMEM(phase_cov.shape, phase_cov.dtype),
                pltpu.VMEM((n_col, width, piece), F32),
                pltpu.VMEM((n_col, width, piece), F32),
                pltpu.VMEM((n_row, (n_row + 1) * block, rank), F32),
                pltpu.VMEM((n_row * block, rank), F32),
                pltpu.VMEM((2, rank, n_row * block // 2), jnp.bfloat16),
                pltpu.VMEM((rank, piece), F32),
                pltpu.VMEM((rank, piece), F32),
                pltpu.VMEM((n_col, out_rows, rank), F32),
                pltpu.VMEM((piece, rank), F32),
                dma, dma((n_col,)), dma((n_col,)),
                dma((chips,)), dma((chips,)),
                dma((n_row, chips + 1)), dma((n_row, chips + 1)), dma((n_row, chips + 1)), dma((n_row, chips + 1)),
                dma, dma, dma((n_col,)), dma((n_col,)),
            ],
            compiler_params=pltpu.CompilerParams(collective_id=0, has_side_effects=True),
        )(right_side, factor_window.T, diag_inverse, phase_cov)
        any_space = pl.BlockSpec(memory_space=pl.ANY)
        return pl.pallas_call(
            store,
            out_shape=tuple(jax.ShapeDtypeStruct(x.shape, x.dtype) for x in found),
            in_specs=[vmem, vmem],
            out_specs=(any_space, any_space),
            scratch_shapes=[dma((2,))],
        )(*(pltpu.with_memory_space_constraint(x, pltpu.VMEM) for x in found))

    in_specs = (P("row", None), P("row", "col"), P("row", None), P("col", "row"))
    out_specs = (P("row", "col", None), P("col", None))
    return jax.shard_map(local, mesh=mesh, in_specs=in_specs, out_specs=out_specs, check_vma=False)
```

```python
import functools

import jax
import jax.numpy as jnp
from jax import lax
from jax.experimental import pallas as pl
from jax.experimental.pallas import tpu as pltpu
from jax.sharding import PartitionSpec as P

MESH = pl.DeviceIdType.MESH
CORES = 2
SUB = 8
F32 = jnp.float32
dot_exact = functools.partial(lax.dot_general, precision=lax.Precision.HIGHEST, preferred_element_type=F32)
NN = (((1,), (0,)), ((), ()))
NT = (((1,), (1,)), ((), ()))


def halves(x):
    high = x.astype(jnp.bfloat16)
    return high, (x - high.astype(F32)).astype(jnp.bfloat16)


def dot_low(a, b):
    return lax.dot_general(a, b, NT, preferred_element_type=F32)


def factor_inverse(gram):
    size = gram.shape[0]
    groups = size // SUB
    parts = [gram[g * SUB:(g + 1) * SUB, :] for g in range(groups)]
    lane = lax.broadcasted_iota(jnp.int32, (SUB, size), 1)
    sub = lax.broadcasted_iota(jnp.int32, (SUB, size), 0)
    spread = lambda x: jnp.broadcast_to(x, (SUB, size))
    out = []
    for g0 in range(groups):
        base = g0 * SUB
        inside = (lane >= base) & (lane < base + SUB)
        cols = [spread(parts[g0][:, base + j:base + j + 1]) for j in range(SUB)]
        entry = {(i, j): spread(cols[j][i:i + 1, :]) for i in range(SUB) for j in range(i + 1)}
        lines = [jnp.where(inside, jnp.where(lane == base + j, 1.0, 0.0), spread(parts[g0][j:j + 1, :])) for j in range(SUB)]
        ratio, inverses = {}, []
        for j in range(SUB):
            inverse = 1.0 / entry[j, j]
            inverses.append(inverse)
            for l in range(j + 1, SUB):
                ratio[l, j] = entry[l, j] * inverse
            for l in range(j + 1, SUB):
                for i in range(l, SUB):
                    entry[i, l] = entry[i, l] - entry[i, j] * ratio[l, j]
                lines[l] = lines[l] - ratio[l, j] * lines[j]
        scaled = [lines[j] * inverses[j] for j in range(SUB)]
        for g in range(g0 + 1, groups):
            left = [spread(parts[g][:, base + j:base + j + 1]) for j in range(SUB)]
            value = jnp.where(inside, 0.0, parts[g])
            for j in range(SUB):
                for l in range(j + 1, SUB):
                    left[l] = left[l] - left[j] * ratio[l, j]
                value = value - left[j] * scaled[j]
            parts[g] = value
        done, pivot = lines[0], entry[0, 0]
        for j in range(1, SUB):
            done = jnp.where(sub == j, lines[j], done)
            pivot = jnp.where(sub == j, entry[j, j], pivot)
        out.append(jnp.where(lane <= sub + base, done * lax.rsqrt(pivot), 0.0))
    return jnp.concatenate(out, axis=0)


def kernel(n_row, n_col, rs_ref, fw_ref, di_ref, cov_ref, basis_ref, solved_ref,
           cov_low, cov32, tile, rows, solved_all, low, part, far_part, bases, wide,
           cov_load, cov_send, cov_recv, f_send, f_recv, x_send, x_recv, p_send, p_recv, s_send, s_recv, b_send, b_recv):
    row = lax.axis_index("row")
    col = lax.axis_index("col")
    chips = n_col // CORES
    chip, core = col // CORES, col % CORES
    partner = chip * CORES + (1 - core)
    mirror = chips - 1 - chip
    side = chip // (chips // 2)
    block = rs_ref.shape[0]
    width = fw_ref.shape[0]
    piece = cov32.shape[2]
    out_rows = bases.shape[1]
    near = n_col // 2

    def summed(q, k):
        return (k == CORES - 1) & (q < chips)

    def needed(i, q):
        return q * CORES * width < i * block

    load = pltpu.make_async_copy(cov_ref, cov_low, cov_load)
    load.start()
    barrier = pltpu.get_barrier_semaphore()
    for d in range(1, n_row):
        pl.semaphore_signal(barrier, inc=1, device_id=(lax.rem(row + d, n_row), col), device_id_type=MESH)
    for d in range(1, n_col):
        pl.semaphore_signal(barrier, inc=1, device_id=(row, lax.rem(col + d, n_col)), device_id_type=MESH)

    di = di_ref[...]
    rows[row, pl.ds(0, block), :] = dot_exact(rs_ref[...].T, di, NT)
    rows[row, pl.ds(block + col * width, width), :] = dot_exact(fw_ref[...], di, NT)
    pl.semaphore_wait(barrier, n_row + n_col - 2)

    def view(i, q, k):
        if isinstance(q, int) and q == chips:
            size = block // CORES
            return rows.at[i, pl.ds(pl.multiple_of(k * size, SUB), size)]
        return rows.at[i, pl.ds(pl.multiple_of(block + (q * CORES + k) * width, SUB), width)]

    def f_copy(q, target, n):
        return pltpu.make_async_remote_copy(
            src_ref=view(row, q, core), dst_ref=view(row, q, core), send_sem=f_send.at[n], recv_sem=f_recv.at[q],
            device_id=(row, target * CORES + core), device_id_type=MESH)

    def x_copy(i, q, d):
        return pltpu.make_async_remote_copy(
            src_ref=view(i, q, core), dst_ref=view(i, q, core), send_sem=x_send.at[d, q], recv_sem=x_recv.at[i, q],
            device_id=(lax.rem(row + d, n_row), col), device_id_type=MESH)

    def p_copy(i, q, k):
        return pltpu.make_async_remote_copy(
            src_ref=view(i, q, k), dst_ref=view(i, q, k), send_sem=p_send.at[i, q], recv_sem=p_recv.at[i, q],
            device_id=(row, partner), device_id_type=MESH)

    far_first = sorted(range(1, n_row), key=lambda d: abs(2 * d - n_row))
    away = sorted(range(1, chips), key=lambda d: abs(2 * d - chips))

    @pl.when(needed(row, chip))
    def _():
        for d in away:
            f_copy(chip, lax.rem(chip + d, chips), d).start()
        for d in far_first:
            x_copy(row, chip, d).start()
        p_copy(row, chip, core).start()
    for d in far_first:
        x_copy(row, chips, d).start()

    def cov_copy(q, k, n):
        via = summed(q, k) & (q // (chips // 2) != side)
        target = jnp.where(via, chips - 1 - q, q) * CORES + k
        slot = lax.rem(col + jnp.where(via, near, 0), n_col)
        return target, pltpu.make_async_remote_copy(
            src_ref=cov32.at[q * CORES + k], dst_ref=tile.at[slot],
            send_sem=cov_send.at[n], recv_sem=cov_recv.at[slot],
            device_id=(row, target), device_id_type=MESH)

    def hop(d):
        return sum(lax.rem(chip // b + d // b, 2) * b for b in (2 ** n for n in range(chips)) if b < chips)

    distant = chips // 2
    steps = [*range(distant, chips), *range(1, distant)]
    order = [(hop(d), k) for d in steps for k in reversed(range(CORES))] + [(chip, 1 - core)]
    cov_sends = [cov_copy(q, k, n) for n, (q, k) in enumerate(order)]
    load.wait()

    def widened(t):
        return cov_low[:, pl.ds(pl.multiple_of(t * piece, piece), piece)].astype(F32)

    for (q, k), (target, copy) in zip(order, cov_sends):
        cov32[q * CORES + k] = widened(q * CORES + k)

        @pl.when(target != col)
        def _():
            copy.start()
    is_summed = summed(chip, core)
    opposite = lax.rem(col + near, n_col)
    tile[col] = widened(col)

    @pl.when(is_summed)
    def _():
        tile[opposite] = cov32[mirror * CORES + core]

    useful = [q for q in reversed(range(chips)) if needed(n_row - 1, q)]
    for q in useful:
        @pl.when(needed(row, q) & (chip != q))
        def _():
            f_copy(q, chip, 0).wait_recv()
            for d in far_first:
                x_copy(row, q, d).start()
            p_copy(row, q, core).start()

    def pieces(i):
        return [chips] + [q for q in useful if needed(i, q)]

    for i in range(n_row):
        @pl.when(row != i)
        def _():
            for q in pieces(i):
                x_copy(i, q, 1).wait_recv()
                p_copy(i, q, core).start()

    solved = []
    for i in range(n_row):
        for q in pieces(i):
            if q < chips:
                p_copy(i, q, 1 - core).wait_recv()
            else:
                @pl.when(row != i)
                def _():
                    p_copy(i, q, 1 - core).wait_recv()

        value = rows[i, pl.ds(0, block), :]
        if i:
            earlier = jnp.concatenate(solved, axis=1) if i > 1 else solved[0]
            value = value - dot_exact(earlier, rows[i, pl.ds(block, i * block), :], NN)
        solved.append(value)
        solved_all[pl.ds(i * block, block), :] = value.T
    middle = n_row // 2
    low[0] = jnp.concatenate(solved[:middle], axis=1).astype(jnp.bfloat16)
    low[1] = jnp.concatenate(solved[middle:], axis=1).astype(jnp.bfloat16)
    solved_ref[...] = solved_all[pl.ds(pl.multiple_of(col * width, width), width), :]

    def contribution(which, base):
        for j in range(near):
            slot = base + j

            @pl.when((slot != col) & jnp.logical_not(is_summed & (slot == opposite)))
            def _():
                pltpu.make_async_remote_copy(
                    src_ref=cov32.at[slot], dst_ref=tile.at[slot], send_sem=cov_send.at[0], recv_sem=cov_recv.at[slot],
                    device_id=(row, partner), device_id_type=MESH).wait_recv()
        whole = tile[pl.ds(base, near)].reshape(near * width, piece).astype(jnp.bfloat16)
        return lax.dot_general(low[which], whole, NN, preferred_element_type=F32)

    extra = jnp.where(is_summed, 1, 0)
    first = lax.rem(side + extra, 2)
    sum_copy = pltpu.make_async_remote_copy(
        src_ref=part, dst_ref=far_part, send_sem=s_send, recv_sem=s_recv,
        device_id=(row, mirror * CORES + core), device_id_type=MESH)
    part[...] = contribution(side, first * near)

    @pl.when(is_summed)
    def _():
        sum_copy.start()

    @pl.when(jnp.logical_not(is_summed))
    def _():
        far_part[...] = part[...]
    rest = contribution(lax.rem(side + 1 - extra, 2), (1 - first) * near)

    @pl.when(is_summed)
    def _():
        sum_copy.wait_recv()
    weighted = rest + far_part[...]
    wide[...] = weighted.T
    inverse = factor_inverse(dot_exact(weighted, weighted, NT))
    inverse_high, inverse_low = halves(inverse)

    def b_copy(source, target, n):
        return pltpu.make_async_remote_copy(
            src_ref=bases.at[target], dst_ref=basis_ref.at[source],
            send_sem=b_send.at[n], recv_sem=b_recv.at[source],
            device_id=(row, target), device_id_type=MESH)

    def basis_rows(targets):
        taken = jnp.concatenate([wide[pl.ds(pl.multiple_of(t * out_rows, out_rows), out_rows), :] for t in targets], axis=0)
        high, low_half = halves(taken)
        found = dot_low(high, inverse_high) + (dot_low(high, inverse_low) + dot_low(low_half, inverse_high))
        return [found[j * out_rows:(j + 1) * out_rows, :] for j in range(len(targets))]

    peers = [hop(d) * CORES + k for d, k in [(d, k) for d in reversed(range(1, chips)) for k in range(CORES)]] + [partner]
    b_sends = []
    for chosen in (peers[:3], peers[3:]):
        found = basis_rows(chosen if chosen[-1] is not peers[-1] else chosen + [col])
        for target, value in zip(chosen, found):
            bases[target] = value
        for target in chosen:
            copy = b_copy(col, target, len(b_sends))
            copy.start()
            b_sends.append(copy)
        if len(found) > len(chosen):
            basis_ref[col] = found[-1]
    for target, copy in cov_sends:
        @pl.when(target != col)
        def _():
            copy.wait_send()

    @pl.when(is_summed)
    def _():
        sum_copy.wait_send()

    @pl.when(needed(row, chip))
    def _():
        for d in away:
            f_copy(chip, chip, d).wait_send()
    for d in far_first:
        x_copy(row, chips, d).wait_send()
    for q in useful:
        @pl.when(needed(row, q))
        def _():
            for d in far_first:
                x_copy(row, q, d).wait_send()
            p_copy(row, q, core).wait_send()
    for i in range(n_row):
        @pl.when(row != i)
        def _():
            for q in pieces(i):
                p_copy(i, q, core).wait_send()
    for n, source in enumerate(peers):
        b_copy(source, col, n).wait_recv()
    for copy in b_sends:
        copy.wait_send()


def store(basis_in, solved_in, basis_out, solved_out, sems):
    first = pltpu.make_async_copy(basis_in, basis_out, sems.at[0])
    second = pltpu.make_async_copy(solved_in, solved_out, sems.at[1])
    first.start()
    second.start()
    first.wait()
    second.wait()


def solution(mesh):
    n_row, n_col = mesh.shape["row"], mesh.shape["col"]

    def local(right_side, factor_window, diag_inverse, phase_cov):
        block, rank = right_side.shape
        width = factor_window.shape[1]
        chips = n_col // CORES
        piece = phase_cov.shape[1] // n_col
        out_rows = piece // n_col
        vmem = pl.BlockSpec(memory_space=pltpu.VMEM)
        dma = pltpu.SemaphoreType.DMA
        found = pl.pallas_call(
            functools.partial(kernel, n_row, n_col),
            out_shape=(
                pltpu.VMEM((n_col, out_rows, rank), F32),
                pltpu.VMEM((width, rank), F32),
            ),
            in_specs=[vmem] * 3 + [pl.BlockSpec(memory_space=pl.ANY)],
            out_specs=(vmem, vmem),
            scratch_shapes=[
                pltpu.VMEM(phase_cov.shape, phase_cov.dtype),
                pltpu.VMEM((n_col, width, piece), F32),
                pltpu.VMEM((n_col, width, piece), F32),
                pltpu.VMEM((n_row, (n_row + 1) * block, rank), F32),
                pltpu.VMEM((n_row * block, rank), F32),
                pltpu.VMEM((2, rank, n_row * block // 2), jnp.bfloat16),
                pltpu.VMEM((rank, piece), F32),
                pltpu.VMEM((rank, piece), F32),
                pltpu.VMEM((n_col, out_rows, rank), F32),
                pltpu.VMEM((piece, rank), F32),
                dma, dma((n_col,)), dma((n_col,)),
                dma((chips,)), dma((chips,)),
                dma((n_row, chips + 1)), dma((n_row, chips + 1)), dma((n_row, chips + 1)), dma((n_row, chips + 1)),
                dma, dma, dma((n_col,)), dma((n_col,)),
            ],
            compiler_params=pltpu.CompilerParams(collective_id=0, has_side_effects=True),
        )(right_side, factor_window.T, diag_inverse, phase_cov)
        any_space = pl.BlockSpec(memory_space=pl.ANY)
        return pl.pallas_call(
            store,
            out_shape=tuple(jax.ShapeDtypeStruct(x.shape, x.dtype) for x in found),
            in_specs=[vmem, vmem],
            out_specs=(any_space, any_space),
            scratch_shapes=[dma((2,))],
        )(*(pltpu.with_memory_space_constraint(x, pltpu.VMEM) for x in found))

    in_specs = (P("row", None), P("row", "col"), P("row", None), P("col", "row"))
    out_specs = (P("row", "col", None), P("col", None))
    return jax.shard_map(local, mesh=mesh, in_specs=in_specs, out_specs=out_specs, check_vma=False)
```

```python
import functools

import jax
import jax.numpy as jnp
from jax import lax
from jax.experimental import pallas as pl
from jax.experimental.pallas import tpu as pltpu
from jax.sharding import PartitionSpec as P

MESH = pl.DeviceIdType.MESH
CORES = 2
SUB = 8
F32 = jnp.float32
dot_exact = functools.partial(lax.dot_general, precision=lax.Precision.HIGHEST, preferred_element_type=F32)
NN = (((1,), (0,)), ((), ()))
NT = (((1,), (1,)), ((), ()))


def halves(x):
    high = x.astype(jnp.bfloat16)
    return high, (x - high.astype(F32)).astype(jnp.bfloat16)


def dot_low(a, b):
    return lax.dot_general(a, b, NT, preferred_element_type=F32)


def factor_inverse(gram):
    size = gram.shape[0]
    groups = size // SUB
    parts = [gram[g * SUB:(g + 1) * SUB, :] for g in range(groups)]
    lane = lax.broadcasted_iota(jnp.int32, (SUB, size), 1)
    sub = lax.broadcasted_iota(jnp.int32, (SUB, size), 0)
    spread = lambda x: jnp.broadcast_to(x, (SUB, size))
    out = []
    for g0 in range(groups):
        base = g0 * SUB
        inside = (lane >= base) & (lane < base + SUB)
        cols = [spread(parts[g0][:, base + j:base + j + 1]) for j in range(SUB)]
        entry = {(i, j): spread(cols[j][i:i + 1, :]) for i in range(SUB) for j in range(i + 1)}
        lines = [jnp.where(inside, jnp.where(lane == base + j, 1.0, 0.0), spread(parts[g0][j:j + 1, :])) for j in range(SUB)]
        ratio, inverses = {}, []
        for j in range(SUB):
            inverse = 1.0 / entry[j, j]
            inverses.append(inverse)
            for l in range(j + 1, SUB):
                ratio[l, j] = entry[l, j] * inverse
            for l in range(j + 1, SUB):
                for i in range(l, SUB):
                    entry[i, l] = entry[i, l] - entry[i, j] * ratio[l, j]
                lines[l] = lines[l] - ratio[l, j] * lines[j]
        scaled = [lines[j] * inverses[j] for j in range(SUB)]
        for g in range(g0 + 1, groups):
            left = [spread(parts[g][:, base + j:base + j + 1]) for j in range(SUB)]
            value = jnp.where(inside, 0.0, parts[g])
            for j in range(SUB):
                for l in range(j + 1, SUB):
                    left[l] = left[l] - left[j] * ratio[l, j]
                value = value - left[j] * scaled[j]
            parts[g] = value
        done, pivot = lines[0], entry[0, 0]
        for j in range(1, SUB):
            done = jnp.where(sub == j, lines[j], done)
            pivot = jnp.where(sub == j, entry[j, j], pivot)
        out.append(jnp.where(lane <= sub + base, done * lax.rsqrt(pivot), 0.0))
    return jnp.concatenate(out, axis=0)


def kernel(n_row, n_col, rs_ref, fw_ref, di_ref, cov_ref, basis_ref, solved_ref,
           cov_low, cov32, tile, rows, solved_all, low, part, far_part, bases, wide,
           cov_load, cov_send, cov_recv, f_send, f_recv, x_send, x_recv, p_send, p_recv, s_send, s_recv, b_send, b_recv):
    row = lax.axis_index("row")
    col = lax.axis_index("col")
    chips = n_col // CORES
    chip, core = col // CORES, col % CORES
    partner = chip * CORES + (1 - core)
    mirror = chips - 1 - chip
    side = chip // (chips // 2)
    block = rs_ref.shape[0]
    width = fw_ref.shape[0]
    piece = cov32.shape[2]
    out_rows = bases.shape[1]
    near = n_col // 2

    def summed(q, k):
        return (k == CORES - 1) & (q < chips)

    def needed(i, q):
        return q * CORES * width < i * block

    load = pltpu.make_async_copy(cov_ref, cov_low, cov_load)
    load.start()
    barrier = pltpu.get_barrier_semaphore()
    for d in range(1, n_row):
        pl.semaphore_signal(barrier, inc=1, device_id=(lax.rem(row + d, n_row), col), device_id_type=MESH)
    for d in range(1, n_col):
        pl.semaphore_signal(barrier, inc=1, device_id=(row, lax.rem(col + d, n_col)), device_id_type=MESH)

    di = di_ref[...]
    rows[row, pl.ds(0, block), :] = dot_exact(rs_ref[...].T, di, NT)
    rows[row, pl.ds(block + col * width, width), :] = dot_exact(fw_ref[...], di, NT)
    pl.semaphore_wait(barrier, n_row + n_col - 2)

    def view(i, q, k):
        if isinstance(q, int) and q == chips:
            size = block // CORES
            return rows.at[i, pl.ds(pl.multiple_of(k * size, SUB), size)]
        return rows.at[i, pl.ds(pl.multiple_of(block + (q * CORES + k) * width, SUB), width)]

    def f_copy(q, target, n):
        return pltpu.make_async_remote_copy(
            src_ref=view(row, q, core), dst_ref=view(row, q, core), send_sem=f_send.at[n], recv_sem=f_recv.at[q],
            device_id=(row, target * CORES + core), device_id_type=MESH)

    def x_copy(i, q, d):
        return pltpu.make_async_remote_copy(
            src_ref=view(i, q, core), dst_ref=view(i, q, core), send_sem=x_send.at[d, q], recv_sem=x_recv.at[i, q],
            device_id=(lax.rem(row + d, n_row), col), device_id_type=MESH)

    def p_copy(i, q, k):
        return pltpu.make_async_remote_copy(
            src_ref=view(i, q, k), dst_ref=view(i, q, k), send_sem=p_send.at[i, q], recv_sem=p_recv.at[i, q],
            device_id=(row, partner), device_id_type=MESH)

    far_first = sorted(range(1, n_row), key=lambda d: abs(2 * d - n_row))
    away = sorted(range(1, chips), key=lambda d: abs(2 * d - chips))

    @pl.when(needed(row, chip))
    def _():
        for d in away:
            f_copy(chip, lax.rem(chip + d, chips), d).start()
        for d in far_first:
            x_copy(row, chip, d).start()
        p_copy(row, chip, core).start()
    for d in far_first:
        x_copy(row, chips, d).start()

    def cov_copy(q, k, n):
        via = summed(q, k) & (q // (chips // 2) != side)
        target = jnp.where(via, chips - 1 - q, q) * CORES + k
        slot = lax.rem(col + jnp.where(via, near, 0), n_col)
        return target, pltpu.make_async_remote_copy(
            src_ref=cov32.at[q * CORES + k], dst_ref=tile.at[slot],
            send_sem=cov_send.at[n], recv_sem=cov_recv.at[slot],
            device_id=(row, target), device_id_type=MESH)

    def hop(d):
        return sum(lax.rem(chip // b + d // b, 2) * b for b in (2 ** n for n in range(chips)) if b < chips)

    distant = chips // 2
    steps = [*range(distant, chips), *range(1, distant)]
    order = [(hop(d), k) for d in steps for k in reversed(range(CORES))] + [(chip, 1 - core)]
    cov_sends = [cov_copy(q, k, n) for n, (q, k) in enumerate(order)]
    load.wait()

    def widened(t):
        return cov_low[:, pl.ds(pl.multiple_of(t * piece, piece), piece)].astype(F32)

    for (q, k), (target, copy) in zip(order, cov_sends):
        cov32[q * CORES + k] = widened(q * CORES + k)

        @pl.when(target != col)
        def _():
            copy.start()
    is_summed = summed(chip, core)
    opposite = lax.rem(col + near, n_col)
    tile[col] = widened(col)

    @pl.when(is_summed)
    def _():
        tile[opposite] = cov32[mirror * CORES + core]

    useful = [q for q in reversed(range(chips)) if needed(n_row - 1, q)]
    for q in useful:
        @pl.when(needed(row, q) & (chip != q))
        def _():
            f_copy(q, chip, 0).wait_recv()
            for d in far_first:
                x_copy(row, q, d).start()
            p_copy(row, q, core).start()

    def pieces(i):
        return [chips] + [q for q in useful if needed(i, q)]

    def forward(i):
        @pl.when(row != i)
        def _():
            for q in pieces(i):
                x_copy(i, q, 1).wait_recv()
                p_copy(i, q, core).start()

    solved = []

    def solve(i):
        for q in pieces(i):
            if q < chips:
                p_copy(i, q, 1 - core).wait_recv()
            else:
                @pl.when(row != i)
                def _():
                    p_copy(i, q, 1 - core).wait_recv()

        value = rows[i, pl.ds(0, block), :]
        if i:
            earlier = jnp.concatenate(solved, axis=1) if i > 1 else solved[0]
            value = value - dot_exact(earlier, rows[i, pl.ds(block, i * block), :], NN)
        solved.append(value)
        solved_all[pl.ds(i * block, block), :] = value.T

    def contribution(which, base):
        for j in range(near):
            slot = base + j

            @pl.when((slot != col) & jnp.logical_not(is_summed & (slot == opposite)))
            def _():
                pltpu.make_async_remote_copy(
                    src_ref=cov32.at[slot], dst_ref=tile.at[slot], send_sem=cov_send.at[0], recv_sem=cov_recv.at[slot],
                    device_id=(row, partner), device_id_type=MESH).wait_recv()
        whole = tile[pl.ds(base, near)].reshape(near * width, piece).astype(jnp.bfloat16)
        return lax.dot_general(low[which], whole, NN, preferred_element_type=F32)

    extra = jnp.where(is_summed, 1, 0)
    first = lax.rem(side + extra, 2)
    sum_copy = pltpu.make_async_remote_copy(
        src_ref=part, dst_ref=far_part, send_sem=s_send, recv_sem=s_recv,
        device_id=(row, mirror * CORES + core), device_id_type=MESH)
    middle = n_row // 2
    early = is_summed & (side == 0)
    for i in range(middle):
        forward(i)
    for i in range(middle):
        solve(i)
    low[0] = jnp.concatenate(solved[:middle], axis=1).astype(jnp.bfloat16)

    @pl.when(early)
    def _():
        part[...] = contribution(0, near)
        sum_copy.start()
    for i in range(middle, n_row):
        forward(i)
    for i in range(middle, n_row):
        solve(i)
    low[1] = jnp.concatenate(solved[middle:], axis=1).astype(jnp.bfloat16)

    @pl.when(jnp.logical_not(early))
    def _():
        part[...] = contribution(side, first * near)

    @pl.when(is_summed & (side == 1))
    def _():
        sum_copy.start()
    solved_ref[...] = solved_all[pl.ds(pl.multiple_of(col * width, width), width), :]

    @pl.when(jnp.logical_not(is_summed))
    def _():
        far_part[...] = part[...]
    rest = contribution(lax.rem(side + 1 - extra, 2), (1 - first) * near)

    @pl.when(is_summed)
    def _():
        sum_copy.wait_recv()
    weighted = rest + far_part[...]
    wide[...] = weighted.T
    inverse = factor_inverse(dot_exact(weighted, weighted, NT))
    inverse_high, inverse_low = halves(inverse)

    def b_copy(source, target, n):
        return pltpu.make_async_remote_copy(
            src_ref=bases.at[target], dst_ref=basis_ref.at[source],
            send_sem=b_send.at[n], recv_sem=b_recv.at[source],
            device_id=(row, target), device_id_type=MESH)

    def basis_rows(targets):
        taken = jnp.concatenate([wide[pl.ds(pl.multiple_of(t * out_rows, out_rows), out_rows), :] for t in targets], axis=0)
        high, low_half = halves(taken)
        found = dot_low(high, inverse_high) + (dot_low(high, inverse_low) + dot_low(low_half, inverse_high))
        return [found[j * out_rows:(j + 1) * out_rows, :] for j in range(len(targets))]

    peers = [hop(d) * CORES + k for d, k in [(d, k) for d in reversed(range(1, chips)) for k in range(CORES)]] + [partner]
    b_sends = []
    for chosen in (peers[:near], peers[near:]):
        found = basis_rows(chosen if len(chosen) == near else chosen + [col])
        for target, value in zip(chosen, found):
            bases[target] = value
        for target in chosen:
            copy = b_copy(col, target, len(b_sends))
            copy.start()
            b_sends.append(copy)
        if len(found) > len(chosen):
            basis_ref[col] = found[-1]
    for target, copy in cov_sends:
        @pl.when(target != col)
        def _():
            copy.wait_send()

    @pl.when(is_summed)
    def _():
        sum_copy.wait_send()

    @pl.when(needed(row, chip))
    def _():
        for d in away:
            f_copy(chip, chip, d).wait_send()
    for d in far_first:
        x_copy(row, chips, d).wait_send()
    for q in useful:
        @pl.when(needed(row, q))
        def _():
            for d in far_first:
                x_copy(row, q, d).wait_send()
            p_copy(row, q, core).wait_send()
    for i in range(n_row):
        @pl.when(row != i)
        def _():
            for q in pieces(i):
                p_copy(i, q, core).wait_send()
    for n, source in enumerate(peers):
        b_copy(source, col, n).wait_recv()
    for copy in b_sends:
        copy.wait_send()


def store(basis_in, solved_in, basis_out, solved_out, sems):
    first = pltpu.make_async_copy(basis_in, basis_out, sems.at[0])
    second = pltpu.make_async_copy(solved_in, solved_out, sems.at[1])
    first.start()
    second.start()
    first.wait()
    second.wait()


def solution(mesh):
    n_row, n_col = mesh.shape["row"], mesh.shape["col"]

    def local(right_side, factor_window, diag_inverse, phase_cov):
        block, rank = right_side.shape
        width = factor_window.shape[1]
        chips = n_col // CORES
        piece = phase_cov.shape[1] // n_col
        out_rows = piece // n_col
        vmem = pl.BlockSpec(memory_space=pltpu.VMEM)
        dma = pltpu.SemaphoreType.DMA
        found = pl.pallas_call(
            functools.partial(kernel, n_row, n_col),
            out_shape=(
                pltpu.VMEM((n_col, out_rows, rank), F32),
                pltpu.VMEM((width, rank), F32),
            ),
            in_specs=[vmem] * 3 + [pl.BlockSpec(memory_space=pl.ANY)],
            out_specs=(vmem, vmem),
            scratch_shapes=[
                pltpu.VMEM(phase_cov.shape, phase_cov.dtype),
                pltpu.VMEM((n_col, width, piece), F32),
                pltpu.VMEM((n_col, width, piece), F32),
                pltpu.VMEM((n_row, (n_row + 1) * block, rank), F32),
                pltpu.VMEM((n_row * block, rank), F32),
                pltpu.VMEM((2, rank, n_row * block // 2), jnp.bfloat16),
                pltpu.VMEM((rank, piece), F32),
                pltpu.VMEM((rank, piece), F32),
                pltpu.VMEM((n_col, out_rows, rank), F32),
                pltpu.VMEM((piece, rank), F32),
                dma, dma((n_col,)), dma((n_col,)),
                dma((chips,)), dma((chips,)),
                dma((n_row, chips + 1)), dma((n_row, chips + 1)), dma((n_row, chips + 1)), dma((n_row, chips + 1)),
                dma, dma, dma((n_col,)), dma((n_col,)),
            ],
            compiler_params=pltpu.CompilerParams(collective_id=0, has_side_effects=True),
        )(right_side, factor_window.T, diag_inverse, phase_cov)
        any_space = pl.BlockSpec(memory_space=pl.ANY)
        return pl.pallas_call(
            store,
            out_shape=tuple(jax.ShapeDtypeStruct(x.shape, x.dtype) for x in found),
            in_specs=[vmem, vmem],
            out_specs=(any_space, any_space),
            scratch_shapes=[dma((2,))],
        )(*(pltpu.with_memory_space_constraint(x, pltpu.VMEM) for x in found))

    in_specs = (P("row", None), P("row", "col"), P("row", None), P("col", "row"))
    out_specs = (P("row", "col", None), P("col", None))
    return jax.shard_map(local, mesh=mesh, in_specs=in_specs, out_specs=out_specs, check_vma=False)
```
